128 devices in a mesh: tm: 32 (over z, y, x_hi), space: 4 (over x_lo, core).
Axes of the slice: x: 4 (x_hi: 2, x_lo: 2; x = x_hi * 2 + x_lo), y: 4, z: 4, core: 2. Of those that a mesh axis runs over, the one named last changes fastest.
Arguments:
- frames: bfloat16 [512, 16, 64, 384], P('tm', 'space'), may hold values from -6 to 6
- token_ids: int32 [1, 512, 16, 64], P(None, 'tm', 'space'), may hold values from 0 to 1023
- action_ids: int32 [512], P('tm'), may hold values from 0 to 7
- token_table: bfloat16 [1024, 384], replicated, may hold values from -6 to 6
- action_table: bfloat16 [8, 384], replicated, may hold values from -3 to 3
- conv_weight: bfloat16 [3, 3, 384], replicated, may hold values from -1.796875 to 1.796875
- norm_gain: bfloat16 [384], replicated, may hold values from 0.5 to 1.5
- w_query: bfloat16 [384, 384], replicated, may hold values from -12 to 12
- w_key: bfloat16 [384, 384], replicated, may hold values from -12 to 12
- w_value: bfloat16 [384, 384], replicated, may hold values from -0.3125 to 0.3125
- w_out: bfloat16 [384, 384], replicated, may hold values from -0.625 to 0.625
Outputs:
- final_frames: bfloat16 [512, 16, 64, 384], P('tm', 'space')
The draws below stay inside these ranges and needn't reach their ends.
All inputs are finite; a program needn't handle non-finite values.
Results may differ from the reference program's by a relative error of at most 0.0057.
Values may be sent and summed in bfloat16 or wider, within the bound.
No kernel may reach another device: no remote copies, remote signals or barrier semaphores. Data moves between devices by JAX's collectives and lax.ppermute only.
A program may use at most 192 MiB of HBM per device.

```python
import jax
import jax.numpy as jnp
from jax import lax

D = 384
HEADS = 6
VOCAB = 1024
ACTIONS = 8
GRID_ROWS = 16
GRID_COLS = 64
WINDOW = 16
ANCHORS = 4
STEPS = 1
FR_DEV = 16
FRAMES = 512


def draw_w_query(key, part):
    random_part = jax.random.normal(jax.random.fold_in(key, 1), (D, D), jnp.float32) / jnp.sqrt(jnp.float32(D))
    return random_part.astype(jnp.bfloat16)


def draw_w_key(key, part):
    random_part = jax.random.normal(jax.random.fold_in(key, 2), (D, D), jnp.float32) / jnp.sqrt(jnp.float32(D))
    return random_part.astype(jnp.bfloat16)


def set_ends(drawn, key, least, top_value):
    shape = drawn.shape
    index_at = [jax.random.randint(jax.random.fold_in(key, axis), (), 0, shape[axis]) for axis in range(len(shape))]
    drawn = drawn.at[tuple(index_at)].set(least)
    longest = shape.index(max(shape))
    index_at[longest] = (index_at[longest] + 1) % shape[longest]
    return drawn.at[tuple(index_at)].set(top_value)


def level_of(own_key, dims, pieces, least, top_value):
    gain = 1.0
    for axis_at, parts in pieces:
        heights = jax.random.uniform(jax.random.fold_in(jax.random.fold_in(own_key, 6), axis_at), (parts,), jnp.float32, least / len(pieces), top_value / len(pieces))
        gain = gain * jnp.repeat(jnp.exp(heights), dims[axis_at] // parts).reshape((-1,) + (1,) * (len(dims) - 1 - axis_at))
    return gain


def noise(key, extent, deviation, reach, shards=(), held_as=jnp.bfloat16):
    drawn = deviation * jax.random.normal(key, extent, jnp.float32)
    if shards:
        drawn = drawn * level_of(key, extent, shards, -0.22, 0.18)
    return jnp.clip(drawn, -reach, reach).astype(held_as)


def setup_inputs(seed: int = 0) -> dict:
    seeds = jax.random.split(jax.random.key(seed), 12)
    return {
        "frames": noise(seeds[0], (FRAMES, GRID_ROWS, GRID_COLS, D), 1.0, 6.0, ((0, 32), (1, 4))),
        "token_ids": set_ends(jax.random.randint(seeds[1], (STEPS, FRAMES, GRID_ROWS, GRID_COLS), 0, VOCAB), jax.random.fold_in(seeds[1], 1), 0, VOCAB - 1).astype(jnp.int32),
        "action_ids": set_ends(jax.random.randint(seeds[2], (FRAMES,), 0, ACTIONS), jax.random.fold_in(seeds[2], 1), 0, ACTIONS - 1).astype(jnp.int32),
        "token_table": noise(seeds[3], (VOCAB, D), 1.0, 6.0),
        "action_table": noise(seeds[4], (ACTIONS, D), 0.5, 3.0),
        "conv_weight": noise(seeds[5], (3, 3, D), 0.3, 1.796875),
        "norm_gain": jnp.clip(1.0 + 0.1 * jax.random.normal(seeds[6], (D,), jnp.float32), 0.5, 1.5).astype(jnp.bfloat16),
        "w_query": draw_w_query(jax.random.fold_in(seeds[11], 71), 0),
        "w_key": draw_w_key(jax.random.fold_in(seeds[11], 71), 0),
        "w_value": noise(seeds[9], (D, D), D ** -0.5, 0.3125),
        "w_out": noise(seeds[10], (D, D), (D // 4) ** -0.5, 0.625),
    }


def attend(queries, keys, values, first_frame, head_count):
    frame_count, positions, width_all = queries.shape
    head_dim = width_all // head_count
    query_frame = first_frame + jnp.arange(frame_count, dtype=jnp.int32)
    key_frame = jnp.concatenate([first_frame - (WINDOW - 1) + jnp.arange(WINDOW - 1 + frame_count, dtype=jnp.int32), jnp.arange(ANCHORS, dtype=jnp.int32)])
    is_anchor = jnp.arange(key_frame.shape[0]) >= WINDOW - 1 + frame_count
    lower = query_frame[:, None] - (WINDOW - 1)
    in_window = (key_frame[None, :] >= 0) & (key_frame[None, :] <= query_frame[:, None]) & (key_frame[None, :] >= lower)
    allowed = jnp.where(is_anchor[None, :], key_frame[None, :] < lower, in_window)
    query_heads = queries.reshape(frame_count, positions, head_count, head_dim).astype(jnp.float32)
    key_heads = keys.reshape(keys.shape[0], positions, head_count, head_dim).astype(jnp.float32)
    value_heads = values.reshape(values.shape[0], positions, head_count, head_dim).astype(jnp.float32)
    scores = jnp.einsum('fphd,kphd->phfk', query_heads, key_heads) / jnp.sqrt(jnp.float32(head_dim))
    scores = jnp.where(allowed[None, None], scores, jnp.float32(-1e+30))
    row_max = lax.optimization_barrier(jnp.max(scores, axis=-1, keepdims=True))
    expo = jnp.exp(scores - row_max)
    probs = (expo / lax.optimization_barrier(jnp.sum(expo, axis=-1, keepdims=True))).astype(jnp.bfloat16)
    attended = jnp.einsum('phfk,kphd->fphd', probs.astype(jnp.float32), value_heads)
    return attended.reshape(frame_count, positions, width_all).astype(jnp.bfloat16)

def reference(frames, token_ids, action_ids, token_table, action_table, conv_weight, norm_gain, w_query, w_key, w_value, w_out):
    frame_total, row_count, col_count, width_all = frames.shape
    positions = row_count * col_count
    onehot = (action_ids[:, None] == jnp.arange(ACTIONS, dtype=jnp.int32)[None, :]).astype(jnp.bfloat16)
    action_rows = jnp.dot(onehot, action_table, preferred_element_type=jnp.float32)
    state = frames
    block_count = frame_total // FR_DEV
    for step_index in range(STEPS):
        token_rows = token_table[token_ids[step_index]]
        embedded = (state.astype(jnp.float32) + token_rows.astype(jnp.float32) + action_rows[:, None, None, :]).astype(jnp.bfloat16)
        padded = jnp.pad(embedded, ((0, 0), (1, 1), (1, 1), (0, 0)))
        mixed = embedded.astype(jnp.float32)
        for row_shift in range(3):
            for col_shift in range(3):
                mixed = mixed + padded[:, row_shift:row_shift + row_count, col_shift:col_shift + col_count, :].astype(jnp.float32) * conv_weight[row_shift, col_shift].astype(jnp.float32)
        scale = lax.rsqrt(lax.optimization_barrier(jnp.mean(mixed * mixed, axis=-1, keepdims=True)) + 1e-06)
        normed = (mixed * scale * norm_gain.astype(jnp.float32)).astype(jnp.bfloat16)
        flat = normed.reshape(frame_total * positions, width_all)
        queries = jnp.dot(flat, w_query, preferred_element_type=jnp.float32).astype(jnp.bfloat16).reshape(frame_total, positions, width_all)
        keys = jnp.dot(flat, w_key, preferred_element_type=jnp.float32).astype(jnp.bfloat16).reshape(frame_total, positions, width_all)
        values = jnp.dot(flat, w_value, preferred_element_type=jnp.float32).astype(jnp.bfloat16).reshape(frame_total, positions, width_all)
        keys_padded = jnp.pad(keys, ((WINDOW - 1, 0), (0, 0), (0, 0)))
        values_padded = jnp.pad(values, ((WINDOW - 1, 0), (0, 0), (0, 0)))

        def one_block(block_index):
            first_frame = (block_index * FR_DEV).astype(jnp.int32)
            query_block = lax.dynamic_slice_in_dim(queries, first_frame, FR_DEV, 0)
            key_block = lax.dynamic_slice_in_dim(keys_padded, first_frame, FR_DEV + WINDOW - 1, 0)
            value_block = lax.dynamic_slice_in_dim(values_padded, first_frame, FR_DEV + WINDOW - 1, 0)
            key_block = jnp.concatenate([key_block, keys[:ANCHORS]], axis=0)
            value_block = jnp.concatenate([value_block, values[:ANCHORS]], axis=0)
            return attend(query_block, key_block, value_block, first_frame, HEADS)
        attended = lax.map(one_block, jnp.arange(block_count, dtype=jnp.int32))
        attended = attended.reshape(frame_total * positions, width_all)
        output = jnp.dot(attended, w_out, preferred_element_type=jnp.float32).reshape(frame_total, row_count, col_count, width_all)
        state = (mixed + output).astype(jnp.bfloat16)
    return state
```

```python
import functools

import jax
import jax.numpy as jnp
from jax import lax
from jax.experimental import pallas as pl
from jax.experimental.pallas import tpu as pltpu
from jax.sharding import PartitionSpec as P

HEADS = 6
ACTIONS = 8
WINDOW = 16
ANCHORS = 4
BF = jnp.bfloat16
F32 = jnp.float32
LOG2E = 1.4426950408889634


def spread(ids_row):
    return jnp.transpose(jnp.broadcast_to(ids_row, (128, 128)))


def lookup(ids, table_ref):
    vocab = table_ref.shape[0]
    lane = lax.broadcasted_iota(jnp.int32, ids.shape, 1)
    pieces = [
        jnp.where(ids == lane + 128 * k, F32(1), F32(0)).astype(BF) for k in range(vocab // 128)
    ]
    onehot = jnp.concatenate(pieces, axis=1)
    return jnp.dot(onehot, table_ref[...], preferred_element_type=F32)


def conv_norm(above, here, below, cw_ref, gain_ref):
    cols = here.shape[0]
    at = lax.broadcasted_iota(jnp.int32, here.shape, 0)

    def part(j):
        return (
            above * cw_ref[j : j + 1, :]
            + here * cw_ref[3 + j : 4 + j, :]
            + below * cw_ref[6 + j : 7 + j, :]
        )

    left = jnp.where(at == 0, F32(0), pltpu.roll(part(0), 1, 0))
    right = jnp.where(at == cols - 1, F32(0), pltpu.roll(part(2), cols - 1, 0))
    mixed = here + part(1) + left + right
    scale = lax.rsqrt(jnp.mean(mixed * mixed, axis=-1, keepdims=True) + 1e-06)
    return mixed, (mixed * scale * gain_ref[...]).astype(BF)


def inner_kernel(
    frames_ref, ids_ref, act_ref, table_ref, cw_ref, gain_ref,
    emb_ref, win_a_ref, win_b_ref, anc_ref, mixed_ref,
):
    f = pl.program_id(0)
    act = act_ref[pl.ds(f, 1), :]
    rows = []
    for half in range(2):
        token = lookup(spread(ids_ref[0, half : half + 1, :]), table_ref)
        for k in range(2):
            r = 2 * half + k
            e = (frames_ref[0, r].astype(F32) + token[64 * k : 64 * k + 64] + act).astype(BF)
            emb_ref[0, r] = e
            rows.append(e.astype(F32))
    for k, win_ref in ((0, win_a_ref), (1, win_b_ref)):
        mixed, normed = conv_norm(rows[k], rows[k + 1], rows[k + 2], cw_ref, gain_ref)
        mixed_ref[0, k] = mixed
        win_ref[0] = normed

        @pl.when(f < ANCHORS)
        def _():
            anc_ref[0, k] = normed


def edge_kernel(
    flag_ref, emb_ref, up_ref, down_ref, ids_ref, act_ref, table_ref, cw_ref, gain_ref,
    win_a_ref, win_b_ref, anc_ref, mixed_ref,
):
    f = pl.program_id(0)
    act = act_ref[pl.ds(f, 1), :]
    token = lookup(spread(ids_ref[0]), table_ref)
    up = (up_ref[0].astype(F32) + token[:64] + act).astype(BF).astype(F32)
    down = (down_ref[0].astype(F32) + token[64:] + act).astype(BF).astype(F32)
    up = jnp.where(flag_ref[0] > 0, up, F32(0))
    down = jnp.where(flag_ref[1] > 0, down, F32(0))
    own = [emb_ref[0, r].astype(F32) for r in range(4)]
    for k, win_ref, three in (
        (0, win_a_ref, (up, own[0], own[1])),
        (1, win_b_ref, (own[2], own[3], down)),
    ):
        mixed, normed = conv_norm(*three, cw_ref, gain_ref)
        mixed_ref[0, k] = mixed
        win_ref[0] = normed

        @pl.when(f < ANCHORS)
        def _():
            anc_ref[0, k] = normed


def attend_kernel(
    first_ref, own0_ref, own_ref, halo_ref, anc_ref, mixed_ref, wqkv_ref, wo_ref, *rest
):
    out_ref, qs, ks, vs, hk, hv, ak, av, att, bias = rest[-10:]
    D = 384
    cols = 64
    first = first_ref[0]
    def put(to, row0, value):
        for j in range(3):
            to[j, pl.ds(row0, value.shape[0]), :] = value[:, 128 * j : 128 * j + 128]

    def qkv(x, row0, q_to, k_to, v_to):
        for i, to in enumerate((q_to, k_to, v_to)):
            if to is not None:
                w = wqkv_ref[:, D * i : D * i + D]
                put(to, row0, jnp.dot(x, w, preferred_element_type=F32))

    qkv(own0_ref[0, 0], 0, qs, ks, vs)
    zero = jnp.zeros((cols, D), F32)
    put(hk, 0, zero)
    put(hv, 0, zero)

    @pl.loop(0, 5)
    def _(i):
        x = own_ref[pl.ds(3 * i, 3)].reshape(3 * cols, D)
        qkv(x, cols + i * 3 * cols, qs, ks, vs)
        x = halo_ref[pl.ds(3 * i, 3)].reshape(3 * cols, D)
        qkv(x, cols + i * 3 * cols, None, hk, hv)

    qkv(anc_ref[:, 0].reshape(ANCHORS * cols, D), 0, None, ak, av)
    for u in range(ANCHORS, 8):
        put(ak, u * cols, zero)
        put(av, u * cols, zero)

    row = lax.broadcasted_iota(jnp.int32, (64, 128), 0)
    col = lax.broadcasted_iota(jnp.int32, (64, 128), 1)
    same = ((row // 8) % 4) == (col // 32)
    key = col % 32
    for half in range(2):
        t = row % 8 + 8 * half
        tail = jnp.where(key < 24, key - 16, 0)
        if half == 0:
            before = key >= t + 1
            before = before & (key < 16)
            own = (key >= 16) & (key < 24) & (tail <= t)
        else:
            own = (key < 16) & (key <= t)
            before = (key >= 16) & (key < 24) & (tail + 8 >= t + 1)
        before = before & (first >= 16)
        anchor = (key >= 24) & (key < 28) & (key - 24 < first + t - (WINDOW - 1))
        ok = same & (own | before | anchor)
        bias[half] = jnp.where(ok, F32(0), F32(-1e30))

    lane = lax.broadcasted_iota(jnp.int32, (32, 128), 1)
    low = lane < 64
    ones = jnp.ones((128, 128), BF)
    c = F32(LOG2E / 8.0)

    @pl.loop(0, cols // 4)
    def _(g):
        p0 = g * 4

        def eight(ref, frame0, p, j):
            return ref[j, pl.ds(frame0 * cols + p0 + p, 8, stride=cols), :]

        for j in range(3):
            qh = [[], []]
            kh = [[], []]
            vh = [[], []]
            for p in range(4):
                for half in range(2):
                    qh[half].append(eight(qs, 8 * half, p, j))
                for src_h, src_o, src_a, to in ((hk, ks, ak, kh), (hv, vs, av, vh)):
                    a_lo, a_hi = eight(src_h, 0, p, j), eight(src_h, 8, p, j)
                    b_lo, b_hi = eight(src_o, 0, p, j), eight(src_o, 8, p, j)
                    anc = eight(src_a, 0, p, j)
                    to[0] += [a_lo, a_hi, b_lo, anc]
                    to[1] += [b_lo, b_hi, a_hi, anc]
            for half in range(2):
                q = jnp.concatenate(qh[half], axis=0).astype(BF)
                k = jnp.concatenate(kh[half], axis=0).astype(BF)
                v = jnp.concatenate(vh[half], axis=0).astype(BF)
                nil = jnp.zeros_like(q)
                qq = jnp.concatenate([jnp.where(low, q, nil), jnp.where(low, nil, q)], axis=0)
                s = lax.dot_general(
                    qq, k, (((1,), (1,)), ((), ())), preferred_element_type=F32
                )
                s = s * c + bias[half]
                e = jnp.exp2(s - jnp.max(s, axis=-1, keepdims=True)).astype(BF)
                o = jnp.dot(e, v, preferred_element_type=F32)
                total = jnp.dot(e, ones, preferred_element_type=F32)
                o = jnp.where(low, o[:32], o[32:]) / jnp.where(low, total[:32], total[32:])
                for p in range(4):
                    at = pl.multiple_of((p0 + p) * 16 + 8 * half, 8)
                    att[pl.ds(at, 8), pl.ds(128 * j, 128)] = o[8 * p : 8 * p + 8]

    @pl.loop(0, 4)
    def _(i):
        x = att[pl.ds(i * 256, 256), :].astype(BF)
        put(qs, i * 256, jnp.dot(x, wo_ref[...], preferred_element_type=F32))

    @pl.loop(0, 16)
    def _(t):
        for j in range(3):
            got = qs[j, pl.ds(t, cols, stride=16), :]
            out_ref[t, 0, :, pl.ds(128 * j, 128)] = (
                mixed_ref[t, 0, :, pl.ds(128 * j, 128)] + got
            ).astype(BF)


def whole(shape):
    return pl.BlockSpec(shape, lambda *_: (0,) * len(shape), pipeline_mode=pl.Buffered(1))


def on_device(
    frames, token_ids, action_ids, token_table, action_table, conv_weight, norm_gain,
    w_query, w_key, w_value, w_out,
):
    F, R, C, D = frames.shape
    tm, sp = lax.axis_index("tm"), lax.axis_index("space")
    n_tm, n_sp = lax.axis_size("tm"), lax.axis_size("space")
    ids = token_ids[0]
    onehot = (action_ids[:, None] == jnp.arange(ACTIONS, dtype=jnp.int32)[None, :]).astype(BF)
    act = jnp.dot(onehot, action_table, preferred_element_type=F32)
    cw = conv_weight.reshape(9, D).astype(F32)
    gain = norm_gain.reshape(1, D).astype(F32)
    wqkv = jnp.concatenate([w_query, w_key, w_value], axis=1)

    up_pairs = [(i, i + 1) for i in range(n_sp - 1)]
    down_pairs = [(j, i) for i, j in up_pairs]
    up = lax.ppermute(frames[:, R - 1], "space", up_pairs)
    down = lax.ppermute(frames[:, 0], "space", down_pairs)
    edge_ids = jnp.concatenate(
        [
            lax.ppermute(ids[:, R - 1], "space", up_pairs),
            lax.ppermute(ids[:, 0], "space", down_pairs),
        ],
        axis=1,
    ).reshape(F, 1, 2 * C)

    common = [whole((F, D)), whole(token_table.shape), whole((9, D)), whole((1, D))]
    win_out = [
        jax.ShapeDtypeStruct((F - 1, C, D), BF),
        jax.ShapeDtypeStruct((F - 1, C, D), BF),
        jax.ShapeDtypeStruct((ANCHORS, 2, C, D), BF),
        jax.ShapeDtypeStruct((F, 2, C, D), F32),
    ]
    win_specs = [
        pl.BlockSpec((1, C, D), lambda f, *_: (jnp.maximum(f - 1, 0), 0, 0)),
        pl.BlockSpec((1, C, D), lambda f, *_: (jnp.maximum(f - 1, 0), 0, 0)),
        pl.BlockSpec((1, 2, C, D), lambda f, *_: (jnp.minimum(f, ANCHORS - 1), 0, 0, 0)),
        pl.BlockSpec((1, 2, C, D), lambda f, *_: (f, 0, 0, 0)),
    ]
    frame_spec = pl.BlockSpec((1, R, C, D), lambda f, *_: (f, 0, 0, 0))
    emb, win1, win2, anc12, mixed12 = pl.pallas_call(
        inner_kernel,
        grid=(F,),
        in_specs=[frame_spec, pl.BlockSpec((1, 2, 128), lambda f: (f, 0, 0))] + common,
        out_specs=[frame_spec] + win_specs,
        out_shape=[jax.ShapeDtypeStruct((F, R, C, D), BF)] + win_out,
        cost_estimate=pl.CostEstimate(
            flops=2 * F * R * C * 1024 * D, bytes_accessed=16 * 2**20, transcendentals=0
        ),
        name="inner",
    )(frames, ids.reshape(F, 2, 128), act, token_table, cw, gain)

    row_spec = pl.BlockSpec((1, C, D), lambda f, *_: (f, 0, 0))
    flags = jnp.stack([sp > 0, sp < n_sp - 1]).astype(jnp.int32)
    win0, win3, anc03, mixed03 = pl.pallas_call(
        edge_kernel,
        grid_spec=pltpu.PrefetchScalarGridSpec(
            num_scalar_prefetch=1,
            grid=(F,),
            in_specs=[
                frame_spec,
                row_spec,
                row_spec,
                pl.BlockSpec((1, 1, 128), lambda f, *_: (f, 0, 0)),
            ]
            + common,
            out_specs=win_specs,
        ),
        out_shape=win_out,
        cost_estimate=pl.CostEstimate(
            flops=F * R * C * 1024 * D, bytes_accessed=16 * 2**20, transcendentals=0
        ),
        name="edge",
    )(flags, emb, up, down, edge_ids, act, token_table, cw, gain)

    shift = [(i, i + 1) for i in range(n_tm - 1)]

    def tree(own):
        held, have = own, [0]
        for by in (1, 4, 2, 16, 8):
            got = lax.ppermute(held, "tm", [(s, s + by) for s in have])
            fresh = [s + by for s in have]
            isnew = functools.reduce(jnp.logical_or, [tm == s for s in fresh])
            held = jnp.where(isnew, got, held)
            have = have + fresh
        return held

    halo1 = lax.ppermute(win1, "tm", shift)
    halo2 = lax.ppermute(win2, "tm", shift)
    all12 = tree(anc12)
    halo0 = lax.ppermute(win0, "tm", shift)
    halo3 = lax.ppermute(win3, "tm", shift)
    all03 = tree(anc03)

    first = (tm * F).astype(jnp.int32).reshape(1)
    out = None
    for r, k, win, halo, anc_own, anc, mixed in (
        (1, 0, win1, halo1, anc12, all12, mixed12),
        (2, 1, win2, halo2, anc12, all12, mixed12),
        (0, 0, win0, halo0, anc03, all03, mixed03),
        (3, 1, win3, halo3, anc03, all03, mixed03),
    ):
        one = dict(pipeline_mode=pl.Buffered(1))
        in_specs = [
            pl.BlockSpec((1, 1, C, D), lambda i, *_, k=k: (0, k, 0, 0), **one),
            whole((F - 1, C, D)),
            whole((F - 1, C, D)),
            pl.BlockSpec((ANCHORS, 1, C, D), lambda i, *_, k=k: (0, k, 0, 0), **one),
            pl.BlockSpec((F, 1, C, D), lambda i, *_, k=k: (0, k, 0, 0), **one),
            whole((D, 3 * D)),
            whole((D, D)),
        ]
        operands = [first, anc_own, win, halo, anc, mixed, wqkv, w_out]
        aliases = {}
        if out is not None:
            in_specs.append(pl.BlockSpec(memory_space=pl.ANY))
            operands.append(out)
            aliases = {8: 0}
        out = pl.pallas_call(
            attend_kernel,
            grid_spec=pltpu.PrefetchScalarGridSpec(
                num_scalar_prefetch=1,
                grid=(1,),
                in_specs=in_specs,
                out_specs=pl.BlockSpec((F, 1, C, D), lambda i, *_, r=r: (0, r, 0, 0), **one),
                scratch_shapes=[pltpu.VMEM((3, F * C, 128), F32)] * 5
                + [pltpu.VMEM((3, 8 * C, 128), F32)] * 2
                + [pltpu.VMEM((F * C, D), F32), pltpu.VMEM((2, 64, 128), F32)],
            ),
            out_shape=jax.ShapeDtypeStruct((F, R, C, D), BF),
            input_output_aliases=aliases,
            cost_estimate=pl.CostEstimate(
                flops=2 * F * C * D * D * 24, bytes_accessed=8 * 2**20, transcendentals=0
            ),
            name="attend",
        )(*operands)
    return out


def solution(mesh):
    in_specs = (
        P("tm", "space", None, None),
        P(None, "tm", "space", None),
        P("tm"),
        P(), P(), P(), P(), P(), P(), P(), P(),
    )
    out_specs = P("tm", "space", None, None)
    return jax.shard_map(
        on_device, mesh=mesh, in_specs=in_specs, out_specs=out_specs, check_vma=False
    )
```

```python
import functools

import jax
import jax.numpy as jnp
from jax import lax
from jax.experimental import pallas as pl
from jax.experimental.pallas import tpu as pltpu
from jax.sharding import PartitionSpec as P

ACTIONS = 8
WINDOW = 16
ANCHORS = 4
BF = jnp.bfloat16
F32 = jnp.float32
LOG2E = 1.4426950408889634


def spread(ids_ref, hi_ref, lo_ref, frame0, count, pair):
    for f in range(count):
        at = slice(frame0 + f, frame0 + f + 1)
        row = jnp.concatenate([ids_ref[0, at, r, :] for r in pair], axis=1)
        wide = jnp.transpose(jnp.broadcast_to(row, (128, 128)))
        hi_ref[pl.ds(128 * f, 128), :] = (wide >> 7).astype(F32).astype(BF)
        lo_ref[pl.ds(128 * f, 128), :] = (wide & 127).astype(F32).astype(BF)


def lookup(hi, lo, table_ref):
    vocab = table_ref.shape[0]
    lane = lax.broadcasted_iota(jnp.int32, lo.shape, 1).astype(F32).astype(BF)
    at_lo = jnp.where(lo == lane, BF(1), BF(0))
    pieces = [jnp.where(hi == BF(k), at_lo, BF(0)) for k in range(vocab // 128)]
    return jnp.dot(jnp.concatenate(pieces, axis=1), table_ref[...], preferred_element_type=F32)


def conv_norm(load, cw_ref, gain_ref, put_mixed, get_mixed, put_normed):
    squares = None
    for j in range(3):
        at = slice(128 * j, 128 * j + 128)
        rows = [load(i, j) for i in range(3)]
        cols = rows[1].shape[0]
        index = lax.broadcasted_iota(jnp.int32, rows[1].shape, 0)

        def part(c):
            return sum(rows[i] * cw_ref[i, c : c + 1, at].astype(F32) for i in range(3))

        mixed = rows[1] + part(1)
        mixed += jnp.where(index == 0, F32(0), pltpu.roll(part(0), 1, 0))
        mixed += jnp.where(index == cols - 1, F32(0), pltpu.roll(part(2), cols - 1, 0))
        put_mixed(j, mixed)
        squares = mixed * mixed if squares is None else squares + mixed * mixed
    scale = lax.rsqrt(jnp.sum(squares, axis=-1, keepdims=True) * F32(1 / 384) + 1e-06)
    for j in range(3):
        put_normed(j, (get_mixed(j) * scale * gain_ref[:, 128 * j : 128 * j + 128].astype(F32)).astype(BF))


def embed_kernel(
    frame0, count, pair, ids_ref, act_ref, table_ref, top_ref, low_ref, a_ref, b_ref, hi, lo
):
    f = pl.program_id(0)

    @pl.when(f == 0)
    def _():
        spread(ids_ref, hi, lo, frame0, count, pair)

    step = top_ref.shape[0]
    at = pl.ds(pl.multiple_of(128 * step * f, 128), 128 * step)
    token = lookup(hi[at, :], lo[at, :], table_ref)
    for i in range(step):
        act = act_ref[pl.ds(frame0 + step * f + i, 1), :]
        for k, ref, to in ((0, top_ref, a_ref), (1, low_ref, b_ref)):
            t = token[128 * i + 64 * k : 128 * i + 64 * k + 64]
            to[i] = (ref[i, 0].astype(F32) + t + act).astype(BF)


def finish(frame0, step, three, cw_ref, gain_ref, held, wins, mixed_ref, anc_ref, rows):
    f0 = pl.program_id(0) * step
    if held:

        @pl.when(f0 == 0)
        def _():
            for old, new in zip(held, wins):
                new[pl.ds(0, frame0 - 1)] = old[...]

    for i in range(step):
        f = frame0 + f0 + i
        for k, win_ref in enumerate(wins):
            def put_mixed(j, value):
                mixed_ref[i, k, :, 128 * j : 128 * j + 128] = value

            def get_mixed(j):
                return mixed_ref[i, k, :, 128 * j : 128 * j + 128]

            def put_normed(j, value):
                at = slice(128 * j, 128 * j + 128)
                win_ref[jnp.maximum(f - 1, 0), :, at] = value
                if anc_ref is not None:
                    anc_ref[f, rows[k], :, at] = value

            conv_norm(
                functools.partial(three, i, k), cw_ref, gain_ref, put_mixed, get_mixed, put_normed
            )


def inner_kernel(
    frame0, count, ids_ref, act_ref, table_ref, top_ref, low_ref, e0_ref, e3_ref, cw_ref, gain_ref,
    *rest
):
    held = rest[:2] if frame0 else ()
    rest = rest[len(held) :]
    e1_ref, e2_ref, win_a_ref, win_b_ref, mixed_ref = rest[:5]
    anc_ref = None if frame0 else rest[5]
    hi, lo = rest[-2:]
    embed_kernel(
        frame0, count, (1, 2), ids_ref, act_ref, table_ref, top_ref, low_ref, e1_ref, e2_ref, hi, lo
    )
    rows = (e0_ref, e1_ref, e2_ref, e3_ref)

    def three(i, k, r, j):
        return rows[k + r][i, :, 128 * j : 128 * j + 128].astype(F32)

    finish(
        frame0, top_ref.shape[0], three, cw_ref, gain_ref, held, (win_a_ref, win_b_ref),
        mixed_ref, anc_ref, (0, 1),
    )


def edge_kernel(
    frame0, last, flag_ref, up_ref, e0_ref, e1_ref, e2_ref, e3_ref, down_ref, cw_ref, gain_ref, *rest
):
    held = rest[:2] if frame0 else ()
    rest = rest[len(held) :]
    win_a_ref, win_b_ref, mixed_ref = rest[:3]
    anc_ref = None if frame0 else rest[3]
    keep = [jnp.where(flag_ref[0] != k, F32(1), F32(0)) for k in (0, last)]
    rows = ((up_ref, e0_ref, e1_ref), (e2_ref, e3_ref, down_ref))

    def three(i, k, r, j):
        row = rows[k][r][i, :, 128 * j : 128 * j + 128].astype(F32)
        return row * keep[k] if r == 2 * k else row

    finish(
        frame0, e0_ref.shape[0], three, cw_ref, gain_ref, held, (win_a_ref, win_b_ref),
        mixed_ref, anc_ref, (0, 1),
    )


def attend_kernel(
    first_ref, own0_ref, own_ref, halo_ref, anc_ref, mix_a_ref, mix_b_ref, wqkv_ref,
    wo_ref, *rest
):
    out_ref, qs, ks, vs, hk, hv, ak, av, att, bias = rest[-10:]
    D = 384
    cols = 64
    first = first_ref[0]
    pitch = cols + 1

    def put(to, row0, value, every=cols, gap=pitch):
        for j in range(3):
            for i in range(value.shape[0] // every):
                piece = value[i * every : i * every + every, 128 * j : 128 * j + 128]
                to[j, pl.ds(row0 + i * gap, every), :] = piece

    def qkv(x, row0, q_to, k_to, v_to):
        for i, to in enumerate((q_to, k_to, v_to)):
            if to is not None:
                w = wqkv_ref[:, D * i : D * i + D]
                put(to, row0, jnp.dot(x, w, preferred_element_type=F32))

    qkv(own0_ref[0, 0], 0, qs, ks, vs)
    zero = jnp.zeros((cols, D), F32)
    put(hk, 0, zero)
    put(hv, 0, zero)

    @pl.loop(0, 3)
    def _(i):
        x = own_ref[pl.ds(5 * i, 5)].reshape(5 * cols, D)
        qkv(x, pitch + i * 5 * pitch, qs, ks, vs)
        x = halo_ref[pl.ds(5 * i, 5)].reshape(5 * cols, D)
        qkv(x, pitch + i * 5 * pitch, None, hk, hv)

    qkv(anc_ref[:, 0].reshape(ANCHORS * cols, D), 0, None, ak, av)
    for u in range(ANCHORS, 8):
        put(ak, u * pitch, zero)
        put(av, u * pitch, zero)

    row = lax.broadcasted_iota(jnp.int32, (64, 128), 0)
    col = lax.broadcasted_iota(jnp.int32, (64, 128), 1)
    same = ((row // 8) % 4) == (col // 32)
    key = col % 32
    for half in range(2):
        t = row % 8 + 8 * half
        tail = jnp.where(key < 24, key - 16, 0)
        if half == 0:
            before = key >= t + 1
            before = before & (key < 16)
            own = (key >= 16) & (key < 24) & (tail <= t)
        else:
            own = (key < 16) & (key <= t)
            before = (key >= 16) & (key < 24) & (tail + 8 >= t + 1)
        before = before & (first >= 16)
        anchor = (key >= 24) & (key < 28) & (key - 24 < first + t - (WINDOW - 1))
        ok = same & (own | before | anchor)
        bias[half] = jnp.where(ok, F32(0), F32(-1e30))

    lane = lax.broadcasted_iota(jnp.int32, (32, 128), 1)
    low = lane < 64
    c = F32(LOG2E / 8.0)

    GROUPS = 4

    @pl.loop(0, cols // (4 * GROUPS))
    def _(g):
        first_col = g * 4 * GROUPS

        def eight(ref, frame0, p, j):
            return ref[j, pl.ds(frame0 * pitch + first_col + p, 8, stride=pitch), :]

        def scores(group, j):
            qh, kh, vh = [[], []], [[], []], [[], []]
            for p in range(4 * group, 4 * group + 4):
                for half in range(2):
                    qh[half].append(eight(qs, 8 * half, p, j))
                for src_h, src_o, src_a, to in ((hk, ks, ak, kh), (hv, vs, av, vh)):
                    a_lo, a_hi = eight(src_h, 0, p, j), eight(src_h, 8, p, j)
                    b_lo, b_hi = eight(src_o, 0, p, j), eight(src_o, 8, p, j)
                    anc = eight(src_a, 0, p, j)
                    to[0] += [a_lo, a_hi, b_lo, anc]
                    to[1] += [b_lo, b_hi, a_hi, anc]
            found = []
            for half in range(2):
                q = jnp.concatenate(qh[half], axis=0).astype(BF)
                k = jnp.concatenate(kh[half], axis=0).astype(BF)
                v = jnp.concatenate(vh[half], axis=0).astype(BF)
                nil = jnp.zeros_like(q)
                qq = jnp.concatenate([jnp.where(low, q, nil), jnp.where(low, nil, q)], axis=0)
                s = lax.dot_general(
                    qq, k, (((1,), (1,)), ((), ())), preferred_element_type=F32
                )
                found.append((group, j, half, s, v))
            return found

        def values(group, j, half, s, v):
            s = s * c + bias[half]
            e = jnp.exp2(s - jnp.max(s, axis=-1, keepdims=True))
            total = jnp.sum(e, axis=-1, keepdims=True)
            o = jnp.dot(e.astype(BF), v, preferred_element_type=F32) / total
            o = jnp.where(low, o[:32], o[32:])
            for p in range(4):
                at = pl.multiple_of((first_col + 4 * group + p) * 16 + 8 * half, 8)
                att[pl.ds(at, 8), pl.ds(128 * j, 128)] = o[8 * p : 8 * p + 8]

        found = []
        for group in range(GROUPS):
            for j in range(3):
                found += scores(group, j)
        for one in found:
            values(*one)

    @pl.loop(0, 4)
    def _(i):
        x = att[pl.ds(i * 256, 256), :].astype(BF)
        put(qs, i * 16 * 17, jnp.dot(x, wo_ref[...], preferred_element_type=F32), 16, 17)

    t0 = 0
    for mixed_ref in (mix_a_ref, mix_b_ref):

        @pl.loop(0, mixed_ref.shape[0])
        def _(i, t0=t0, mixed_ref=mixed_ref):
            t = t0 + i
            for j in range(3):
                got = qs[j, pl.ds(t, cols, stride=17), :]
                out_ref[t, 0, :, pl.ds(128 * j, 128)] = (
                    mixed_ref[i, 0, :, pl.ds(128 * j, 128)] + got
                ).astype(BF)

        t0 += mixed_ref.shape[0]


def whole(shape):
    return pl.BlockSpec(shape, lambda *_: (0,) * len(shape), pipeline_mode=pl.Buffered(1))


def on_device(
    frames, token_ids, action_ids, token_table, action_table, conv_weight, norm_gain,
    w_query, w_key, w_value, w_out,
):
    F, R, C, D = frames.shape
    tm, sp = lax.axis_index("tm"), lax.axis_index("space")
    n_tm, n_sp = lax.axis_size("tm"), lax.axis_size("space")
    onehot = (action_ids[:, None] == jnp.arange(ACTIONS, dtype=jnp.int32)[None, :]).astype(BF)
    act = jnp.dot(onehot, action_table, preferred_element_type=F32)
    cw, gain = conv_weight, norm_gain.reshape(1, D)
    wqkv = jnp.concatenate([w_query, w_key, w_value], axis=1)

    up_pairs = [(i, i + 1) for i in range(n_sp - 1)]
    down_pairs = [(j, i) for i, j in up_pairs]
    step = 2
    parts = ((0, 4), (4, 12))
    table_specs = [whole((1, F, R, C)), whole((F, D)), whole(token_table.shape)]
    conv_specs = [whole((3, 3, D)), whole((1, D))]

    def row_of(r, f0=0):
        return pl.BlockSpec((step, 1, C, D), lambda f, *_: (f0 // step + f, r, 0, 0))

    line = pl.BlockSpec((step, C, D), lambda f, *_: (f, 0, 0))
    pair = pl.BlockSpec((step, 2, C, D), lambda f, *_: (f, 0, 0, 0))

    def shape(n, *k):
        return jax.ShapeDtypeStruct((n, *k, C, D), BF)

    def cost(us):
        return pl.CostEstimate(flops=int(us * 4e8), bytes_accessed=int(us * 1e5), transcendentals=0)

    flags = sp.astype(jnp.int32).reshape(1)
    edges = []
    for (f0, n) in parts:
        e0, e3 = pl.pallas_call(
            functools.partial(embed_kernel, f0, n, (0, R - 1)),
            grid=(n // step,),
            in_specs=table_specs + [row_of(0, f0), row_of(R - 1, f0)],
            out_specs=[line] * 2,
            out_shape=[shape(n)] * 2,
            scratch_shapes=[pltpu.VMEM((n * 2 * C, 128), BF)] * 2,
            cost_estimate=cost(n / 2),
            name="embed",
        )(token_ids, act, token_table, frames, frames)
        up = lax.ppermute(e3, "space", up_pairs)
        down = lax.ppermute(e0, "space", down_pairs)
        edges.append((e0, e3, up, down))

    def win_outs(f0, n):
        so_far = f0 + n - 1
        return (
            [shape(so_far)] * 2 + [jax.ShapeDtypeStruct((n, 2, C, D), F32)],
            [whole((so_far, C, D))] * 2 + [pair],
        )

    inner, mids, mixed12 = [], [], []
    for p, (f0, n) in enumerate(parts):
        shapes, specs = win_outs(f0, n)
        in_specs = table_specs + [row_of(1, f0), row_of(2, f0), line, line] + conv_specs
        operands = [token_ids, act, token_table, frames, frames, *edges[p][:2], cw, gain]
        if f0:
            in_specs += [whole((f0 - 1, C, D))] * 2
            operands += inner[-1][:2]
        else:
            shapes = shapes + [shape(ANCHORS, 2)]
            specs = specs + [whole((ANCHORS, 2, C, D))]
        e1, e2, *rest = pl.pallas_call(
            functools.partial(inner_kernel, f0, n),
            grid=(n // step,),
            in_specs=in_specs,
            out_specs=[line] * 2 + specs,
            out_shape=[shape(n)] * 2 + shapes,
            scratch_shapes=[pltpu.VMEM((n * 2 * C, 128), BF)] * 2,
            cost_estimate=cost(n),
            name="inner",
        )(*operands)
        mids.append((e1, e2))
        inner.append(rest)
        mixed12.append(rest[2])

    outer, mixed03 = [], []
    for p, (f0, n) in enumerate(parts):
        shapes, specs = win_outs(f0, n)
        e0, e3, up, down = edges[p]
        in_specs = [line] * 6 + conv_specs
        operands = [flags, up, e0, *mids[p], e3, down, cw, gain]
        if f0:
            in_specs += [whole((f0 - 1, C, D))] * 2
            operands += outer[-1][:2]
        else:
            shapes = shapes + [shape(ANCHORS, 2)]
            specs = specs + [whole((ANCHORS, 2, C, D))]
        rest = pl.pallas_call(
            functools.partial(edge_kernel, f0, n_sp - 1),
            grid_spec=pltpu.PrefetchScalarGridSpec(
                num_scalar_prefetch=1,
                grid=(n // step,),
                in_specs=in_specs,
                out_specs=specs,
            ),
            out_shape=shapes,
            cost_estimate=cost(n),
            name="edge",
        )(*operands)
        outer.append(rest)
        mixed03.append(rest[2])

    own_anchors = {"a": inner[0][3], "b": outer[0][3]}
    held = dict(own_anchors)
    have = {k: [0] for k in range(n_sp)}
    z, y = tm // 8, tm // 2 % 4
    even = sp % 2 == 0
    a, b = jnp.where(even, z, y), jnp.where(even, y, z)
    fresh = [tm == 1, (a == 2) & (b == 0), (a % 2 == 1) & (b == 0), b == 3, b == 2, b == 1]

    def moves_of(n, k, holders):
        a_by, b_by = (8, 2) if k % 2 == 0 else (2, 8)
        if n == 0:
            return [(t, t + 1) for t in holders]
        if n == 1:
            return [(t, t + 2 * a_by) for t in holders]
        if n == 2:
            return [(t, t + 3 * a_by if t // a_by % 4 == 0 else t - a_by) for t in holders]
        if n == 3:
            return [(t, t + 3 * b_by) for t in holders]
        return [(t, t - b_by) for t in holders if t // b_by % 4 == 7 - n]

    for n in range(6):
        moves = [(t, to, k) for k in range(n_sp) for t, to in moves_of(n, k, have[k])]
        for _, to, k in moves:
            have[k] = have[k] + [to]
        pairs = [(t * n_sp + k, to * n_sp + k) for t, to, k in moves]
        for tree in "ab":
            got = lax.ppermute(held[tree], ("tm", "space"), pairs)
            held[tree] = jnp.where(fresh[n], got, held[tree])

    shift = [(i, i + 1) for i in range(n_tm - 1)]
    wins = {1: inner[-1][0], 2: inner[-1][1], 0: outer[-1][0], 3: outer[-1][1]}
    halos = {}
    for r in (1, 2, 0, 3):
        halos[r] = lax.ppermute(wins[r], "tm", shift)

    first = (tm * F).astype(jnp.int32).reshape(1)
    out = None
    for r in (1, 2, 0, 3):
        if r in (1, 2):
            k, mixed, tree = r - 1, mixed12, "a"
        else:
            k, mixed, tree = r // 3, mixed03, "b"
        one = dict(pipeline_mode=pl.Buffered(1))
        in_specs = [
            pl.BlockSpec((1, 1, C, D), lambda i, *_, k=k: (0, k, 0, 0), **one),
            whole((F - 1, C, D)),
            whole((F - 1, C, D)),
            pl.BlockSpec((ANCHORS, 1, C, D), lambda i, *_, k=k: (0, k, 0, 0), **one),
        ]
        in_specs += [
            pl.BlockSpec((n, 1, C, D), lambda i, *_, k=k: (0, k, 0, 0), **one) for _, n in parts
        ]
        in_specs += [whole((D, 3 * D)), whole((D, D))]
        operands = [
            first, own_anchors[tree], wins[r], halos[r], held[tree], *mixed, wqkv, w_out
        ]
        aliases = {}
        if out is not None:
            in_specs.append(pl.BlockSpec(memory_space=pl.ANY))
            operands.append(out)
            aliases = {len(operands) - 1: 0}
        out = pl.pallas_call(
            attend_kernel,
            grid_spec=pltpu.PrefetchScalarGridSpec(
                num_scalar_prefetch=1,
                grid=(1,),
                in_specs=in_specs,
                out_specs=pl.BlockSpec((F, 1, C, D), lambda i, *_, r=r: (0, r, 0, 0), **one),
                scratch_shapes=[pltpu.VMEM((3, 17 * (C + 1), 128), F32)] * 5
                + [pltpu.VMEM((3, 8 * (C + 1), 128), F32)] * 2
                + [pltpu.VMEM((F * C, D), F32), pltpu.VMEM((2, 64, 128), F32)],
            ),
            out_shape=jax.ShapeDtypeStruct((F, R, C, D), BF),
            input_output_aliases=aliases,
            cost_estimate=cost(10),
            name="attend",
        )(*operands)
    return out


def solution(mesh):
    in_specs = (
        P("tm", "space", None, None),
        P(None, "tm", "space", None),
        P("tm"),
        P(), P(), P(), P(), P(), P(), P(), P(),
    )
    out_specs = P("tm", "space", None, None)

    return jax.shard_map(
        on_device, mesh=mesh, in_specs=in_specs, out_specs=out_specs, check_vma=False
    )
```

```python
import functools

import jax
import jax.numpy as jnp
from jax import lax
from jax.experimental import pallas as pl
from jax.experimental.pallas import tpu as pltpu
from jax.sharding import PartitionSpec as P

WINDOW = 16
ANCHORS = 4
BF = jnp.bfloat16
F32 = jnp.float32
LOG2E = 1.4426950408889634


def spread(ids_ref, hi_ref, lo_ref, frame0, count, pair):
    for f in range(count):
        at = slice(frame0 + f, frame0 + f + 1)
        row = jnp.concatenate([ids_ref[0, at, r, :] for r in pair], axis=1)
        wide = jnp.transpose(jnp.broadcast_to(row, (128, 128)))
        hi_ref[pl.ds(128 * f, 128), :] = (wide >> 7).astype(F32).astype(BF)
        lo_ref[pl.ds(128 * f, 128), :] = (wide & 127).astype(F32).astype(BF)


def lookup(hi, lo, table_ref):
    vocab = table_ref.shape[0]
    lane = lax.broadcasted_iota(jnp.int32, lo.shape, 1).astype(F32).astype(BF)
    at_lo = jnp.where(lo == lane, BF(1), BF(0))
    pieces = [jnp.where(hi == BF(k), at_lo, BF(0)) for k in range(vocab // 128)]
    return jnp.dot(jnp.concatenate(pieces, axis=1), table_ref[...], preferred_element_type=F32)


def conv_norm(load, cw_ref, gain_ref, put_mixed, get_mixed, put_normed):
    squares = None
    for j in range(3):
        at = slice(128 * j, 128 * j + 128)
        rows = [load(i, j) for i in range(3)]
        cols = rows[1].shape[0]
        index = lax.broadcasted_iota(jnp.int32, rows[1].shape, 0)

        def part(c):
            return sum(rows[i] * cw_ref[i, c : c + 1, at].astype(F32) for i in range(3))

        mixed = rows[1] + part(1)
        mixed += jnp.where(index == 0, F32(0), pltpu.roll(part(0), 1, 0))
        mixed += jnp.where(index == cols - 1, F32(0), pltpu.roll(part(2), cols - 1, 0))
        put_mixed(j, mixed)
        squares = mixed * mixed if squares is None else squares + mixed * mixed
    scale = lax.rsqrt(jnp.sum(squares, axis=-1, keepdims=True) * F32(1 / 384) + 1e-06)
    for j in range(3):
        put_normed(j, (get_mixed(j) * scale * gain_ref[:, 128 * j : 128 * j + 128].astype(F32)).astype(BF))


def embed_kernel(
    frame0, count, pair, action_ref, ids_ref, act_ref, table_ref, top_ref, low_ref, a_ref, b_ref,
    hi, lo,
):
    f = pl.program_id(0)

    @pl.when(f == 0)
    def _():
        spread(ids_ref, hi, lo, frame0, count, pair)

    step = top_ref.shape[0]
    at = pl.ds(pl.multiple_of(128 * step * f, 128), 128 * step)
    token = lookup(hi[at, :], lo[at, :], table_ref)
    actions = act_ref[...].astype(F32)
    index = lax.broadcasted_iota(jnp.int32, actions.shape, 0)
    for i in range(step):
        picked = index == action_ref[frame0 + step * f + i]
        act = jnp.sum(jnp.where(picked, actions, F32(0)), axis=0, keepdims=True)
        for k, ref, to in ((0, top_ref, a_ref), (1, low_ref, b_ref)):
            t = token[128 * i + 64 * k : 128 * i + 64 * k + 64]
            to[i] = (ref[i, 0].astype(F32) + t + act).astype(BF)


def finish(frame0, step, three, cw_ref, gain_ref, held, wins, mixed_ref, anc_ref, rows):
    f0 = pl.program_id(0) * step
    if held:

        @pl.when(f0 == 0)
        def _():
            for old, new in zip(held, wins):
                new[pl.ds(0, frame0 - 1)] = old[...]

    for i in range(step):
        f = frame0 + f0 + i
        for k, win_ref in enumerate(wins):
            def put_mixed(j, value):
                mixed_ref[i, k, :, 128 * j : 128 * j + 128] = value

            def get_mixed(j):
                return mixed_ref[i, k, :, 128 * j : 128 * j + 128]

            def put_normed(j, value):
                at = slice(128 * j, 128 * j + 128)
                win_ref[jnp.maximum(f - 1, 0), :, at] = value
                if anc_ref is not None:
                    anc_ref[f, rows[k], :, at] = value

            conv_norm(
                functools.partial(three, i, k), cw_ref, gain_ref, put_mixed, get_mixed, put_normed
            )


def inner_kernel(
    frame0, count, action_ref, ids_ref, act_ref, table_ref, top_ref, low_ref, e0_ref, e3_ref, cw_ref,
    gain_ref, *rest
):
    held = rest[:2] if frame0 else ()
    rest = rest[len(held) :]
    e1_ref, e2_ref, win_a_ref, win_b_ref, mixed_ref = rest[:5]
    anc_ref = None if frame0 else rest[5]
    hi, lo = rest[-2:]
    embed_kernel(
        frame0, count, (1, 2), action_ref, ids_ref, act_ref, table_ref, top_ref, low_ref, e1_ref,
        e2_ref, hi, lo,
    )
    rows = (e0_ref, e1_ref, e2_ref, e3_ref)

    def three(i, k, r, j):
        return rows[k + r][i, :, 128 * j : 128 * j + 128].astype(F32)

    finish(
        frame0, top_ref.shape[0], three, cw_ref, gain_ref, held, (win_a_ref, win_b_ref),
        mixed_ref, anc_ref, (0, 1),
    )


def edge_kernel(
    frame0, last, flag_ref, up_ref, e0_ref, e1_ref, e2_ref, e3_ref, down_ref, cw_ref, gain_ref, *rest
):
    held = rest[:2] if frame0 else ()
    rest = rest[len(held) :]
    win_a_ref, win_b_ref, mixed_ref = rest[:3]
    anc_ref = None if frame0 else rest[3]
    keep = [jnp.where(flag_ref[0] != k, F32(1), F32(0)) for k in (0, last)]
    rows = ((up_ref, e0_ref, e1_ref), (e2_ref, e3_ref, down_ref))

    def three(i, k, r, j):
        row = rows[k][r][i, :, 128 * j : 128 * j + 128].astype(F32)
        return row * keep[k] if r == 2 * k else row

    finish(
        frame0, e0_ref.shape[0], three, cw_ref, gain_ref, held, (win_a_ref, win_b_ref),
        mixed_ref, anc_ref, (0, 1),
    )


def attend_kernel(
    first_ref, own0_ref, own_ref, halo_ref, anc_ref, mix_a_ref, mix_b_ref, mix_c_ref, wq_ref,
    wk_ref, wv_ref, wo_ref, *rest
):
    out_ref, qs, ks, vs, hk, hv, ak, av, att, bias = rest[-10:]
    D = 384
    cols = 64
    first = first_ref[0]
    pitch = cols + 1

    def put(to, row0, value, every=cols, gap=pitch):
        for j in range(3):
            for i in range(value.shape[0] // every):
                piece = value[i * every : i * every + every, 128 * j : 128 * j + 128]
                to[j, pl.ds(row0 + i * gap, every), :] = piece

    def qkv(x, row0, q_to, k_to, v_to):
        for w_ref, to in ((wq_ref, q_to), (wk_ref, k_to), (wv_ref, v_to)):
            if to is not None:
                put(to, row0, jnp.dot(x, w_ref[...], preferred_element_type=F32))

    qkv(own0_ref[0, 0], 0, qs, ks, vs)
    zero = jnp.zeros((cols, D), F32)
    put(hk, 0, zero)
    put(hv, 0, zero)

    @pl.loop(0, 3)
    def _(i):
        x = own_ref[pl.ds(5 * i, 5)].reshape(5 * cols, D)
        qkv(x, pitch + i * 5 * pitch, qs, ks, vs)
        x = halo_ref[pl.ds(5 * i, 5)].reshape(5 * cols, D)
        qkv(x, pitch + i * 5 * pitch, None, hk, hv)

    qkv(anc_ref[:, 0].reshape(ANCHORS * cols, D), 0, None, ak, av)
    for u in range(ANCHORS, 8):
        put(ak, u * pitch, zero)
        put(av, u * pitch, zero)

    row = lax.broadcasted_iota(jnp.int32, (64, 128), 0)
    col = lax.broadcasted_iota(jnp.int32, (64, 128), 1)
    same = ((row // 8) % 4) == (col // 32)
    key = col % 32
    for half in range(2):
        t = row % 8 + 8 * half
        tail = jnp.where(key < 24, key - 16, 0)
        if half == 0:
            before = key >= t + 1
            before = before & (key < 16)
            own = (key >= 16) & (key < 24) & (tail <= t)
        else:
            own = (key < 16) & (key <= t)
            before = (key >= 16) & (key < 24) & (tail + 8 >= t + 1)
        before = before & (first >= 16)
        anchor = (key >= 24) & (key < 28) & (key - 24 < first + t - (WINDOW - 1))
        ok = same & (own | before | anchor)
        bias[half] = jnp.where(ok, F32(0), F32(-1e30))

    lane = lax.broadcasted_iota(jnp.int32, (32, 128), 1)
    low = lane < 64
    c = F32(LOG2E / 8.0)

    GROUPS = 8

    @pl.loop(0, cols // (4 * GROUPS))
    def _(g):
        first_col = g * 4 * GROUPS

        def eight(ref, frame0, p, j):
            return ref[j, pl.ds(frame0 * pitch + first_col + p, 8, stride=pitch), :]

        def scores(group, j):
            qh, kh, vh = [[], []], [[], []], [[], []]
            for p in range(4 * group, 4 * group + 4):
                for half in range(2):
                    qh[half].append(eight(qs, 8 * half, p, j))
                for src_h, src_o, src_a, to in ((hk, ks, ak, kh), (hv, vs, av, vh)):
                    a_lo, a_hi = eight(src_h, 0, p, j), eight(src_h, 8, p, j)
                    b_lo, b_hi = eight(src_o, 0, p, j), eight(src_o, 8, p, j)
                    anc = eight(src_a, 0, p, j)
                    to[0] += [a_lo, a_hi, b_lo, anc]
                    to[1] += [b_lo, b_hi, a_hi, anc]
            found = []
            for half in range(2):
                q = jnp.concatenate(qh[half], axis=0).astype(BF)
                k = jnp.concatenate(kh[half], axis=0).astype(BF)
                v = jnp.concatenate(vh[half], axis=0).astype(BF)
                nil = jnp.zeros_like(q)
                qq = jnp.concatenate([jnp.where(low, q, nil), jnp.where(low, nil, q)], axis=0)
                s = lax.dot_general(
                    qq, k, (((1,), (1,)), ((), ())), preferred_element_type=F32
                )
                found.append((group, j, half, s, v))
            return found

        def values(group, j, half, s, v):
            s = s * c + bias[half]
            e = jnp.exp2(s - jnp.max(s, axis=-1, keepdims=True))
            total = jnp.sum(e, axis=-1, keepdims=True)
            o = jnp.dot(e.astype(BF), v, preferred_element_type=F32) / total
            o = jnp.where(low, o[:32], o[32:])
            for p in range(4):
                at = pl.multiple_of((first_col + 4 * group + p) * 16 + 8 * half, 8)
                att[pl.ds(at, 8), pl.ds(128 * j, 128)] = o[8 * p : 8 * p + 8]

        found = []
        for group in range(GROUPS):
            for j in range(3):
                found += scores(group, j)
        for one in found:
            values(*one)

    @pl.loop(0, 4)
    def _(i):
        x = att[pl.ds(i * 256, 256), :].astype(BF)
        put(qs, i * 16 * 17, jnp.dot(x, wo_ref[...], preferred_element_type=F32), 16, 17)

    t0 = 0
    for mixed_ref in (mix_a_ref, mix_b_ref, mix_c_ref):

        @pl.loop(0, mixed_ref.shape[0])
        def _(i, t0=t0, mixed_ref=mixed_ref):
            t = t0 + i
            for j in range(3):
                got = qs[j, pl.ds(t, cols, stride=17), :]
                out_ref[t, 0, :, pl.ds(128 * j, 128)] = (
                    mixed_ref[i, 0, :, pl.ds(128 * j, 128)] + got
                ).astype(BF)

        t0 += mixed_ref.shape[0]


def whole(shape):
    return pl.BlockSpec(shape, lambda *_: (0,) * len(shape), pipeline_mode=pl.Buffered(1))


def on_device(
    frames, token_ids, action_ids, token_table, action_table, conv_weight, norm_gain,
    w_query, w_key, w_value, w_out,
):
    F, R, C, D = frames.shape
    tm, sp = lax.axis_index("tm"), lax.axis_index("space")
    n_tm, n_sp = lax.axis_size("tm"), lax.axis_size("space")
    cw, gain = conv_weight, norm_gain.reshape(1, D)

    up_pairs = [(i, i + 1) for i in range(n_sp - 1)]
    down_pairs = [(j, i) for i, j in up_pairs]
    step = 2
    early = ((0, 4), (4, 12))
    parts = ((0, 4), (4, 6), (10, 6))
    table_specs = [
        pl.BlockSpec(memory_space=pltpu.SMEM),
        whole((1, F, R, C)),
        whole(action_table.shape),
        whole(token_table.shape),
    ]
    conv_specs = [whole((3, 3, D)), whole((1, D))]

    def row_of(r, f0=0):
        return pl.BlockSpec((step, 1, C, D), lambda f, *_: (f0 // step + f, r, 0, 0))

    def line_of(f0=0):
        return pl.BlockSpec((step, C, D), lambda f, *_: (f0 // step + f, 0, 0))

    line = line_of()
    pair = pl.BlockSpec((step, 2, C, D), lambda f, *_: (f, 0, 0, 0))

    def shape(n, *k):
        return jax.ShapeDtypeStruct((n, *k, C, D), BF)

    def cost(us):
        return pl.CostEstimate(flops=int(us * 4e8), bytes_accessed=int(us * 1e5), transcendentals=0)

    flags = sp.astype(jnp.int32).reshape(1)
    edges = []
    for (f0, n) in early:
        e0, e3 = pl.pallas_call(
            functools.partial(embed_kernel, f0, n, (0, R - 1)),
            grid=(n // step,),
            in_specs=table_specs + [row_of(0, f0), row_of(R - 1, f0)],
            out_specs=[line] * 2,
            out_shape=[shape(n)] * 2,
            scratch_shapes=[pltpu.VMEM((n * 2 * C, 128), BF)] * 2,
            cost_estimate=cost(n / 2),
            name="embed",
        )(action_ids, token_ids, action_table, token_table, frames, frames)
        up = lax.ppermute(e3, "space", up_pairs)
        down = lax.ppermute(e0, "space", down_pairs)
        edges.append((e0, e3, up, down))

    def win_outs(f0, n):
        so_far = f0 + n - 1
        return (
            [shape(so_far)] * 2 + [jax.ShapeDtypeStruct((n, 2, C, D), F32)],
            [whole((so_far, C, D))] * 2 + [pair],
        )

    inner, mids, mixed12 = [], [], []
    for p, (f0, n) in enumerate(parts):
        shapes, specs = win_outs(f0, n)
        in_specs = table_specs + [row_of(1, f0), row_of(2, f0)] + [line_of(f0 - early[min(p, 1)][0])] * 2 + conv_specs
        operands = [action_ids, token_ids, action_table, token_table, frames, frames]
        operands += [*edges[min(p, 1)][:2], cw, gain]
        if f0:
            in_specs += [whole((f0 - 1, C, D))] * 2
            operands += inner[-1][:2]
        else:
            shapes = shapes + [shape(ANCHORS, 2)]
            specs = specs + [whole((ANCHORS, 2, C, D))]
        e1, e2, *rest = pl.pallas_call(
            functools.partial(inner_kernel, f0, n),
            grid=(n // step,),
            in_specs=in_specs,
            out_specs=[line] * 2 + specs,
            out_shape=[shape(n)] * 2 + shapes,
            scratch_shapes=[pltpu.VMEM((n * 2 * C, 128), BF)] * 2,
            cost_estimate=cost(n),
            name="inner",
        )(*operands)
        mids.append((e1, e2))
        inner.append(rest)
        mixed12.append(rest[2])

    outer, mixed03 = [], []
    for p, (f0, n) in enumerate(parts):
        shapes, specs = win_outs(f0, n)
        e0, e3, up, down = edges[min(p, 1)]
        far = line_of(f0 - early[min(p, 1)][0])
        in_specs = [far, far, line, line, far, far] + conv_specs
        operands = [flags, up, e0, *mids[p], e3, down, cw, gain]
        if f0:
            in_specs += [whole((f0 - 1, C, D))] * 2
            operands += outer[-1][:2]
        else:
            shapes = shapes + [shape(ANCHORS, 2)]
            specs = specs + [whole((ANCHORS, 2, C, D))]
        rest = pl.pallas_call(
            functools.partial(edge_kernel, f0, n_sp - 1),
            grid_spec=pltpu.PrefetchScalarGridSpec(
                num_scalar_prefetch=1,
                grid=(n // step,),
                in_specs=in_specs,
                out_specs=specs,
            ),
            out_shape=shapes,
            cost_estimate=cost(n),
            name="edge",
        )(*operands)
        outer.append(rest)
        mixed03.append(rest[2])

    own_anchors = {"a": inner[0][3], "b": outer[0][3]}
    held = dict(own_anchors)
    have = {k: [0] for k in range(n_sp)}
    z, y = tm // 8, tm // 2 % 4
    even = sp % 2 == 0
    a, b = jnp.where(even, z, y), jnp.where(even, y, z)
    fresh = [tm == 1, (a == 2) & (b == 0), (a % 2 == 1) & (b == 0), b == 3, b == 2, b == 1]

    def moves_of(n, k, holders):
        a_by, b_by = (8, 2) if k % 2 == 0 else (2, 8)
        if n == 0:
            return [(t, t + 1) for t in holders]
        if n == 1:
            return [(t, t + 2 * a_by) for t in holders]
        if n == 2:
            return [(t, t + 3 * a_by if t // a_by % 4 == 0 else t - a_by) for t in holders]
        if n == 3:
            return [(t, t + 3 * b_by) for t in holders]
        return [(t, t - b_by) for t in holders if t // b_by % 4 == 7 - n]

    for n in range(6):
        moves = [(t, to, k) for k in range(n_sp) for t, to in moves_of(n, k, have[k])]
        for _, to, k in moves:
            have[k] = have[k] + [to]
        pairs = [(t * n_sp + k, to * n_sp + k) for t, to, k in moves]
        for tree in "ab":
            got = lax.ppermute(held[tree], ("tm", "space"), pairs)
            held[tree] = jnp.where(fresh[n], got, held[tree])

    shift = [(i, i + 1) for i in range(n_tm - 1)]
    wins = {1: inner[-1][0], 2: inner[-1][1], 0: outer[-1][0], 3: outer[-1][1]}
    halos = {}
    for r in (1, 2, 0, 3):
        halos[r] = lax.ppermute(wins[r], "tm", shift)

    first = (tm * F).astype(jnp.int32).reshape(1)
    out = None
    for r in (1, 2, 0, 3):
        if r in (1, 2):
            k, mixed, tree = r - 1, mixed12, "a"
        else:
            k, mixed, tree = r // 3, mixed03, "b"
        one = dict(pipeline_mode=pl.Buffered(1))
        in_specs = [
            pl.BlockSpec((1, 1, C, D), lambda i, *_, k=k: (0, k, 0, 0), **one),
            whole((F - 1, C, D)),
            whole((F - 1, C, D)),
            pl.BlockSpec((ANCHORS, 1, C, D), lambda i, *_, k=k: (0, k, 0, 0), **one),
        ]
        in_specs += [
            pl.BlockSpec((n, 1, C, D), lambda i, *_, k=k: (0, k, 0, 0), **one) for _, n in parts
        ]
        in_specs += [whole((D, D))] * 4
        operands = [
            first, own_anchors[tree], wins[r], halos[r], held[tree], *mixed, w_query,
            w_key, w_value, w_out,
        ]
        aliases = {}
        if out is not None:
            in_specs.append(pl.BlockSpec(memory_space=pl.ANY))
            operands.append(out)
            aliases = {len(operands) - 1: 0}
        out = pl.pallas_call(
            attend_kernel,
            grid_spec=pltpu.PrefetchScalarGridSpec(
                num_scalar_prefetch=1,
                grid=(1,),
                in_specs=in_specs,
                out_specs=pl.BlockSpec((F, 1, C, D), lambda i, *_, r=r: (0, r, 0, 0), **one),
                scratch_shapes=[pltpu.VMEM((3, 17 * (C + 1), 128), F32)] * 5
                + [pltpu.VMEM((3, 8 * (C + 1), 128), F32)] * 2
                + [pltpu.VMEM((F * C, D), F32), pltpu.VMEM((2, 64, 128), F32)],
            ),
            out_shape=jax.ShapeDtypeStruct((F, R, C, D), BF),
            input_output_aliases=aliases,
            cost_estimate=cost(10),
            name="attend",
        )(*operands)
    return out


def solution(mesh):
    in_specs = (
        P("tm", "space", None, None),
        P(None, "tm", "space", None),
        P("tm"),
        P(), P(), P(), P(), P(), P(), P(), P(),
    )
    out_specs = P("tm", "space", None, None)

    return jax.shard_map(
        on_device, mesh=mesh, in_specs=in_specs, out_specs=out_specs, check_vma=False
    )
```
